256 devices in a mesh: file: 8 (over x, core), blk: 32 (over z, y).
Axes of the slice: x: 4, y: 4, z: 8, core: 2. Of those that a mesh axis runs over, the one named last changes fastest.
Arguments:
- ctx_keys: bfloat16 [32768, 256], P(('file', 'blk')), parts along dimension 0, may hold values from -4 to 4
- ctx_values: bfloat16 [32768, 256], P(('file', 'blk')), parts along dimension 0, may hold values from -6 to 6
- middle_queries: bfloat16 [32768, 1792], P(('file', 'blk')), parts along dimension 0, may hold values from -40 to 40
- span_keys: bfloat16 [32768, 256], P(('file', 'blk')), parts along dimension 0, may hold values from -6 to 6
- span_values: bfloat16 [32768, 256], P(('file', 'blk')), parts along dimension 0, may hold values from -6 to 6
- span_len: int32 [256], P(('file', 'blk')), parts along dimension 0, may hold values from 36 to 128, as said below
- commit_pos: int32 [256, 2, 16], P(('file', 'blk')), parts along dimension 0, may hold values from 4 to 127, as said below
- commit_emb: bfloat16 [256, 2, 16, 3584], P(('file', 'blk')), parts along dimension 0, may hold values from -6 to 6
- w_key: bfloat16 [3584, 256], replicated, may hold values from -0.09375 to 0.09375
- w_value: bfloat16 [3584, 256], replicated, may hold values from -0.09375 to 0.09375
Outputs:
- span_out: bfloat16 [2, 32768, 1792], P(None, ('file', 'blk')), parts along dimension 1
The draws below stay inside these ranges and needn't reach their ends.
There are 8 independent parts, one for each index of `file`. The reference program is written for one: setup_inputs(seed, part) draws one part's arguments, and reference() takes and returns one part's arrays. A program takes and returns all parts, laid end to end along the dimension named above; an argument that names none is the same for every part. Nothing has to cross between parts.
Inputs may be any that keep to these rules, and one draw needn't show every extreme that they name: `span_len`: some device's span fills all 128 slots in every draw. `commit_pos`: each device commits exactly 16 slots a step; a device's committed slots are distinct over all steps and lie below that device's span length.
All inputs are finite; a program needn't handle non-finite values.
Results may differ from the reference program's by a relative error of at most 0.0067.
Values may be sent and summed in bfloat16 or wider, within the bound.
No kernel may reach another device: no remote copies, remote signals or barrier semaphores. Data moves between devices by JAX's collectives and lax.ppermute only.
A program may use at most 256 MiB of HBM per device.

```python
import math
import jax
import jax.numpy as jnp
from jax import lax

D = 3584
HEAD_WIDTH = 128
KEY_VALUE_HEADS = 2
STEPS = 2
COMMIT = 16
SPAN_DEV = 128
QUERY_PER_KEY = 7
QUERY_FEATURES = 1792
KVW = 256
FILE = 4096
SPAN = 4096
N_BLK = 32


def context_rows(key):
    rows_of_keys = jnp.clip(jax.random.normal(jax.random.fold_in(key, 11), (FILE, KVW), jnp.float32), -4.0, 4.0)
    return rows_of_keys


def draw_ctx_keys(key, part):
    return context_rows(key).astype(jnp.bfloat16)


def draw_middle_queries(key, part):
    query_matrix = jnp.clip(2.5 * jax.random.normal(jax.random.fold_in(key, 12), (SPAN, QUERY_FEATURES), jnp.float32), -10.0, 10.0)
    return query_matrix.astype(jnp.bfloat16)


def span_plan(key):
    shortest = 4 + STEPS * COMMIT
    lengths = jax.random.randint(jax.random.fold_in(key, 21), (N_BLK,), shortest, SPAN_DEV + 1)
    full_device = jax.random.randint(jax.random.fold_in(key, 22), (), 0, N_BLK)
    lengths = jnp.where(jnp.arange(N_BLK) == full_device, SPAN_DEV, lengths).astype(jnp.int32)
    subkeys = jax.random.split(jax.random.fold_in(key, 23), N_BLK)
    shuffled = jax.vmap(lambda subkey: jax.random.permutation(subkey, SPAN_DEV))(subkeys)
    slots = jnp.arange(SPAN_DEV)
    excluded = (slots[None, :] < 4) | (slots[None, :] >= lengths[:, None])
    scores = shuffled + excluded.astype(jnp.int32) * SPAN_DEV
    selected_index = jnp.argsort(scores, axis=1, stable=True)[:, :STEPS * COMMIT]
    return (lengths, selected_index.reshape(N_BLK, STEPS, COMMIT).astype(jnp.int32))


def draw_span_len(key, part):
    return span_plan(key)[0]


def draw_commit_pos(key, part):
    return span_plan(key)[1]


def levels(key, dims, pieces, low, top_value):
    def one(position, shards_of):
        steps = jax.random.uniform(jax.random.fold_in(jax.random.fold_in(key, 6), position), (shards_of,), jnp.float32, low / len(pieces), top_value / len(pieces))
        return jnp.repeat(jnp.exp(steps), dims[position] // shards_of).reshape((-1,) + (1,) * (len(dims) - position - 1))

    factor_of = one(*pieces[0])
    for cut in pieces[1:]:
        factor_of = factor_of * one(*cut)
    return factor_of


def scatter_about(own_key, dims, scale, bound, cuts=(), kind=jnp.bfloat16):
    result = jax.random.normal(own_key, dims, jnp.float32) * scale
    if len(cuts) > 0:
        result = levels(own_key, dims, cuts, -0.22, 0.18) * result
    return jnp.clip(result, min=-bound, max=bound).astype(kind)


def setup_inputs(seed: int = 0, part: int = 0) -> dict:
    splits = jax.random.split(jax.random.key(seed), 11)
    part_splits = jax.random.split(jax.random.fold_in(splits[10], part), 11)
    return {
        "ctx_keys": draw_ctx_keys(jax.random.fold_in(jax.random.fold_in(splits[10], part), 71), part),
        "ctx_values": scatter_about(part_splits[1], (FILE, KVW), 1.0, 6.0, ((0, 32),)),
        "middle_queries": draw_middle_queries(jax.random.fold_in(jax.random.fold_in(splits[10], part), 71), part),
        "span_keys": scatter_about(part_splits[3], (SPAN, KVW), 1.0, 6.0, ((0, 32),)),
        "span_values": scatter_about(part_splits[4], (SPAN, KVW), 1.0, 6.0, ((0, 32),)),
        "span_len": draw_span_len(jax.random.fold_in(jax.random.fold_in(splits[10], part), 71), part),
        "commit_pos": draw_commit_pos(jax.random.fold_in(jax.random.fold_in(splits[10], part), 71), part),
        "commit_emb": scatter_about(part_splits[7], (N_BLK, STEPS, COMMIT, D), 1.0, 6.0, ((0, 32),)),
        "w_key": scatter_about(splits[8], (D, KVW), D ** -0.5, 0.09375),
        "w_value": scatter_about(splits[9], (D, KVW), D ** -0.5, 0.09375),
    }


def attend(query_matrix, key_matrix, value_matrix, live_keys, active):
    token_rows = query_matrix.shape[0]
    heads_of_queries = query_matrix.astype(jnp.float32).reshape(token_rows, KEY_VALUE_HEADS, QUERY_PER_KEY, HEAD_WIDTH)
    attention_outputs = []
    for head_group in range(KEY_VALUE_HEADS):
        key_head = key_matrix[:, head_group * HEAD_WIDTH:(head_group + 1) * HEAD_WIDTH].astype(jnp.float32)
        value_head = value_matrix[:, head_group * HEAD_WIDTH:(head_group + 1) * HEAD_WIDTH].astype(jnp.float32)
        scores = jnp.einsum('srd,kd->srk', heads_of_queries[:, head_group], key_head) / math.sqrt(HEAD_WIDTH)
        scores = jnp.where(live_keys[None, None, :], scores, -jnp.inf)
        row_max = lax.optimization_barrier(jnp.max(scores, axis=-1, keepdims=True))
        expw = jnp.exp(scores - row_max)
        total = lax.optimization_barrier(jnp.sum(expw, axis=-1, keepdims=True))
        weights = lax.optimization_barrier(expw.astype(jnp.bfloat16))
        numer = jnp.einsum('srk,kd->srd', weights.astype(jnp.float32), value_head)
        attention_outputs.append(numer / total)
    attention_output = jnp.stack(attention_outputs, axis=1).reshape(token_rows, KEY_VALUE_HEADS * QUERY_PER_KEY * HEAD_WIDTH)
    return jnp.where(active[:, None], attention_output, 0.0).astype(jnp.bfloat16)

def reference(ctx_keys, ctx_values, middle_queries, span_keys, span_values, span_len, commit_pos, commit_emb, w_key, w_value):
    slots = jnp.arange(SPAN_DEV, dtype=jnp.int32)
    live_span = slots[None, :] < span_len[:, None]
    live_keys = jnp.concatenate([jnp.ones((FILE,), bool), live_span.reshape(SPAN)])
    keys_now = span_keys
    values_now = span_values
    committed = jnp.zeros((N_BLK, SPAN_DEV), bool)
    attention_outputs = []
    for number in range(STEPS):
        embedded = commit_emb[:, number].reshape(N_BLK * COMMIT, D)
        new_keys = jnp.dot(embedded, w_key, preferred_element_type=jnp.float32).astype(jnp.bfloat16)
        new_values = jnp.dot(embedded, w_value, preferred_element_type=jnp.float32).astype(jnp.bfloat16)
        slot_ids = commit_pos[:, number]
        row_ids = (jnp.arange(N_BLK, dtype=jnp.int32)[:, None] * SPAN_DEV + slot_ids).reshape(-1).astype(jnp.int32)
        keys_now = keys_now.at[row_ids].set(new_keys)
        values_now = values_now.at[row_ids].set(new_values)
        committed = committed | jnp.any(slots[None, None, :] == slot_ids[:, :, None], axis=1)
        active = (live_span & ~committed).reshape(SPAN)
        attention_outputs.append(attend(middle_queries, jnp.concatenate([ctx_keys, keys_now]), jnp.concatenate([ctx_values, values_now]), live_keys, active))
    return jnp.stack(attention_outputs)
```

```python
import functools
import math

import jax
import jax.numpy as jnp
from jax import lax
from jax.experimental import pallas as pl
from jax.experimental.pallas import tpu as pltpu
from jax.sharding import PartitionSpec as P

BF16 = jnp.bfloat16
F32 = jnp.float32
HEAD = 128
GROUPS = 2
PER_GROUP = 7
HEADS = GROUPS * PER_GROUP
COMMIT = 16
SLOTS = 128
COMMON = SLOTS - COMMIT
BOTH = SLOTS - 2 * COMMIT
KVW = GROUPS * HEAD
PAIR = 2 * KVW
ROWS = PER_GROUP * COMMON
MARK = 1e30
SCALE = math.log2(math.e) / math.sqrt(HEAD)
VMEM = pl.BlockSpec(memory_space=pltpu.VMEM)
SMEM = pl.BlockSpec(memory_space=pltpu.SMEM)


def vmem_params(mib):
    return pltpu.CompilerParams(vmem_limit_bytes=mib << 20)


def named_slots(pos_ref, step):
    slot = lax.broadcasted_iota(jnp.int32, (SLOTS, COMMIT), 0)
    return (slot == pos_ref[0, step : step + 1, :]).astype(F32)


def rank_of(flag):
    row = lax.broadcasted_iota(jnp.int32, (SLOTS, SLOTS), 0)
    col = lax.broadcasted_iota(jnp.int32, (SLOTS, SLOTS), 1)
    return jnp.dot((col < row).astype(BF16), flag.astype(BF16), preferred_element_type=F32)


def lanes():
    return lax.broadcasted_iota(jnp.int32, (SLOTS, SLOTS), 1).astype(F32)


def flag_of(named):
    return jnp.broadcast_to(jnp.max(named, axis=1, keepdims=True), (SLOTS, SLOTS))


def select_rows(chosen, rows):
    return lax.dot_general(
        chosen.astype(BF16), rows, (((0,), (0,)), ((), ())), preferred_element_type=F32
    ).astype(BF16)


def span_rows(len_ref, pos_ref, emb_ref, wk_ref, wv_ref, sk_ref, sv_ref, out_ref, base):
    named0 = named_slots(pos_ref, 0)
    named1 = named_slots(pos_ref, 1)
    in0 = flag_of(named0)
    stay = 1.0 - flag_of(named1)
    chosen = jnp.where(rank_of(stay) == lanes(), stay, 0.0)
    dead = lax.broadcasted_iota(jnp.int32, (SLOTS, KVW), 0) >= len_ref[0]
    emb = emb_ref[0].reshape(2 * COMMIT, emb_ref.shape[3])
    for part, (w_ref, s_ref) in enumerate(((wk_ref, sk_ref), (wv_ref, sv_ref))):
        new = jnp.dot(emb, w_ref[...], preferred_element_type=F32).astype(BF16)
        put = jnp.dot(named0.astype(BF16), new[:COMMIT], preferred_element_type=F32)
        now = jnp.where(
            jnp.concatenate([in0, in0], axis=1) > 0.5, put, s_ref[...].astype(F32)
        )
        filler = now[0:1, :] if part == 0 else jnp.full((1, KVW), MARK, F32)
        now = jnp.where(dead, filler, now).astype(BF16)
        cols = slice(part * KVW, (part + 1) * KVW)
        out_ref[base : base + COMMON, cols] = select_rows(chosen, now)[:COMMON]
        out_ref[base + COMMON : base + SLOTS, cols] = select_rows(named1, now)
        out_ref[base + SLOTS : base + SLOTS + COMMIT, cols] = new[COMMIT:]


def prepare_kernel(
    len_ref, pos_ref, emb_ref, wk_ref, wv_ref, ck_ref, cv_ref, sk_ref, sv_ref, out_ref
):
    out_ref[0:SLOTS, 0:KVW] = ck_ref[...]
    out_ref[0:SLOTS, KVW:PAIR] = cv_ref[...]
    span_rows(len_ref, pos_ref, emb_ref, wk_ref, wv_ref, sk_ref, sv_ref, out_ref, SLOTS)


def query_order(pos_ref):
    in0 = flag_of(named_slots(pos_ref, 0))
    in1 = flag_of(named_slots(pos_ref, 1))
    never = (1.0 - in0) * (1.0 - in1)
    first = jnp.where(rank_of(never) == lanes(), never, 0.0)
    second = jnp.where(rank_of(in1) + float(BOTH) == lanes(), in1, 0.0)
    return first, second


def queries_kernel(pos_ref, mq_ref, out_ref):
    first, second = query_order(pos_ref)
    picked = select_rows(first + second, mq_ref[...])
    for head in range(HEADS):
        out_ref[head * COMMON : (head + 1) * COMMON, :] = picked[
            :COMMON, head * HEAD : (head + 1) * HEAD
        ]


def attend(q, keys, values, old_acc, old_max):
    marked = values > MARK / 2
    zero = jnp.zeros_like(values)
    values = jnp.concatenate(
        [jnp.where(marked, zero, values), jnp.where(marked, zero, jnp.ones_like(values))], axis=1
    )
    scores = lax.dot_general(q, keys, (((1,), (1,)), ((), ())), preferred_element_type=F32)
    new_max = jnp.maximum(old_max, jnp.max(scores, axis=1, keepdims=True))
    weights = jnp.exp2((scores - new_max[:, :1]) * SCALE).astype(BF16)
    keep = jnp.exp2((old_max - new_max) * SCALE)
    gained = jnp.dot(weights, values, preferred_element_type=F32)
    return old_acc * jnp.concatenate([keep, keep], axis=1) + gained, new_max


def head_cols(group, part):
    return slice(part * KVW + group * HEAD, part * KVW + (group + 1) * HEAD)


def attention_kernel(
    blocks, len_ref, pos_ref, q_ref, kv_ref, out_ref, acc, top, shared, old, new, rows_out
):
    step = pl.program_id(0)
    size = SLOTS + COMMON

    @pl.when(step == 0)
    def _():
        acc[...] = jnp.zeros_like(acc)
        top[...] = jnp.full_like(top, -1e30)

    for b in range(blocks):
        at = b * (2 * SLOTS + COMMIT)
        shared[b * size : (b + 1) * size, :] = kv_ref[at : at + size, :]
        where = pl.ds(pl.multiple_of((step * blocks + b) * COMMIT, COMMIT), COMMIT)
        old[where, :] = kv_ref[at + size : at + 2 * SLOTS, :]
        new[where, :] = kv_ref[at + 2 * SLOTS : at + 2 * SLOTS + COMMIT, :]

    for group in range(GROUPS):
        for head in range(PER_GROUP):
            at = (group * PER_GROUP + head) * COMMON
            rows = slice(at, at + COMMON)
            acc[rows, :], top[rows, :] = attend(
                q_ref[rows, :],
                shared[:, head_cols(group, 0)],
                shared[:, head_cols(group, 1)],
                acc[rows, :],
                top[rows, :],
            )

    @pl.when(step == pl.num_programs(0) - 1)
    def _():
        first, second = query_order(pos_ref)
        live = lax.broadcasted_iota(jnp.int32, (SLOTS, SLOTS), 0) < len_ref[0]
        rows_out[COMMON:, :] = jnp.zeros((COMMIT, HEADS * HEAD), BF16)
        for number, extra in enumerate((old, new)):
            for group in range(GROUPS):
                for head in range(PER_GROUP):
                    index = group * PER_GROUP + head
                    rows = slice(index * COMMON, (index + 1) * COMMON)
                    full, _ = attend(
                        q_ref[rows, :],
                        extra[:, head_cols(group, 0)],
                        extra[:, head_cols(group, 1)],
                        acc[rows, :],
                        top[rows, :],
                    )
                    rows_out[:COMMON, index * HEAD : (index + 1) * HEAD] = (
                        full[:, :HEAD] / full[:, HEAD:]
                    ).astype(BF16)
            place = jnp.where(live, first + second if number == 0 else first, 0.0).astype(BF16)
            out_ref[number] = jnp.dot(
                place, rows_out[...], preferred_element_type=F32
            ).astype(BF16)


def per_device(
    ctx_keys,
    ctx_values,
    middle_queries,
    span_keys,
    span_values,
    span_len,
    commit_pos,
    commit_emb,
    w_key,
    w_value,
):
    payload = pl.pallas_call(
        prepare_kernel,
        out_shape=jax.ShapeDtypeStruct((2 * SLOTS + COMMIT, PAIR), BF16),
        in_specs=[SMEM] + [VMEM] * 8,
        out_specs=VMEM,
        compiler_params=vmem_params(24),
        name="prepare",
    )(
        span_len,
        commit_pos,
        commit_emb,
        w_key,
        w_value,
        ctx_keys,
        ctx_values,
        span_keys,
        span_values,
    )
    gathered = lax.all_gather(payload, "blk", axis=0, tiled=True)
    queries = pl.pallas_call(
        queries_kernel,
        out_shape=jax.ShapeDtypeStruct((HEADS * COMMON, HEAD), BF16),
        in_specs=[VMEM, VMEM],
        out_specs=VMEM,
        compiler_params=vmem_params(24),
        name="queries",
    )(commit_pos, middle_queries)
    count = gathered.shape[0] // payload.shape[0]
    blocks = 8
    whole = lambda shape: pl.BlockSpec(shape, lambda i: (0,) * len(shape))
    return pl.pallas_call(
        functools.partial(attention_kernel, blocks),
        out_shape=jax.ShapeDtypeStruct((2, SLOTS, HEADS * HEAD), BF16),
        grid=(count // blocks,),
        in_specs=[
            SMEM,
            whole(commit_pos.shape),
            whole(queries.shape),
            pl.BlockSpec((blocks * payload.shape[0], PAIR), lambda i: (i, 0)),
        ],
        out_specs=whole((2, SLOTS, HEADS * HEAD)),
        scratch_shapes=[
            pltpu.VMEM((HEADS * COMMON, 2 * HEAD), F32),
            pltpu.VMEM((HEADS * COMMON, HEAD), F32),
            pltpu.VMEM((blocks * (SLOTS + COMMON), PAIR), BF16),
            pltpu.VMEM((count * COMMIT, PAIR), BF16),
            pltpu.VMEM((count * COMMIT, PAIR), BF16),
            pltpu.VMEM((SLOTS, HEADS * HEAD), BF16),
        ],
        compiler_params=vmem_params(50),
        name="attention",
    )(span_len, commit_pos, queries, gathered)


def solution(mesh):
    both = ("file", "blk")
    in_specs = (
        P(both, None),
        P(both, None),
        P(both, None),
        P(both, None),
        P(both, None),
        P(both),
        P(both, None, None),
        P(both, None, None, None),
        P(),
        P(),
    )
    return jax.shard_map(
        per_device, mesh=mesh, in_specs=in_specs, out_specs=P(None, both, None), check_vma=False
    )
```

```python
import functools
import math

import jax
import jax.numpy as jnp
from jax import lax
from jax.experimental import pallas as pl
from jax.experimental.pallas import tpu as pltpu
from jax.sharding import PartitionSpec as P

BF16 = jnp.bfloat16
F32 = jnp.float32
HEAD = 128
GROUPS = 2
PER_GROUP = 7
HEADS = GROUPS * PER_GROUP
COMMIT = 16
SLOTS = 128
COMMON = SLOTS - COMMIT
BOTH = SLOTS - 2 * COMMIT
KVW = GROUPS * HEAD
PAIR = 2 * KVW
ROWS = PER_GROUP * COMMON
MARK = 1e30
SCALE = math.log2(math.e) / math.sqrt(HEAD)
VMEM = pl.BlockSpec(memory_space=pltpu.VMEM)
SMEM = pl.BlockSpec(memory_space=pltpu.SMEM)


def vmem_params(mib):
    return pltpu.CompilerParams(vmem_limit_bytes=mib << 20)


def named_slots(pos_ref, step):
    slot = lax.broadcasted_iota(jnp.int32, (SLOTS, COMMIT), 0)
    return (slot == pos_ref[0, step : step + 1, :]).astype(F32)


def rank_of(flag):
    row = lax.broadcasted_iota(jnp.int32, (SLOTS, SLOTS), 0)
    col = lax.broadcasted_iota(jnp.int32, (SLOTS, SLOTS), 1)
    return jnp.dot((col < row).astype(BF16), flag.astype(BF16), preferred_element_type=F32)


def lanes():
    return lax.broadcasted_iota(jnp.int32, (SLOTS, SLOTS), 1).astype(F32)


def flag_of(named):
    return jnp.broadcast_to(jnp.max(named, axis=1, keepdims=True), (SLOTS, SLOTS))


def select_rows(chosen, rows):
    return lax.dot_general(
        chosen.astype(BF16), rows, (((0,), (0,)), ((), ())), preferred_element_type=F32
    ).astype(BF16)


def join_kernel(keys_ref, values_ref, out_ref, sems):
    copies = [
        pltpu.make_async_copy(keys_ref, out_ref.at[:, pl.ds(0, KVW)], sems.at[0]),
        pltpu.make_async_copy(values_ref, out_ref.at[:, pl.ds(KVW, KVW)], sems.at[1]),
    ]
    for copy in copies:
        copy.start()
    for copy in copies:
        copy.wait()


def prepare_kernel(len_ref, pos_ref, *refs):
    sources, out_ref, held, sems = refs[:5], refs[5], refs[6:11], refs[11]
    copies = [
        pltpu.make_async_copy(source, target, sems.at[i])
        for i, (source, target) in enumerate(zip(sources, held))
    ]
    for copy in copies:
        copy.start()
    emb_ref, wk_ref, wv_ref, sk_ref, sv_ref = held
    named0 = named_slots(pos_ref, 0)
    named1 = named_slots(pos_ref, 1)
    in0 = flag_of(named0)
    stay = 1.0 - flag_of(named1)
    chosen = jnp.where(rank_of(stay) == lanes(), stay, 0.0)
    dead = lax.broadcasted_iota(jnp.int32, (SLOTS, KVW), 0) >= len_ref[0]
    for part, (w_ref, s_ref) in enumerate(((wk_ref, sk_ref), (wv_ref, sv_ref))):
        if part == 0:
            copies[0].wait()
        copies[1 + part].wait()
        copies[3 + part].wait()
        emb = emb_ref[0].reshape(2 * COMMIT, emb_ref.shape[3])
        new = jnp.dot(emb, w_ref[...], preferred_element_type=F32).astype(BF16)
        put = jnp.dot(named0.astype(BF16), new[:COMMIT], preferred_element_type=F32)
        now = jnp.where(
            jnp.concatenate([in0, in0], axis=1) > 0.5, put, s_ref[...].astype(F32)
        )
        filler = now[0:1, :] if part == 0 else jnp.full((1, KVW), MARK, F32)
        now = jnp.where(dead, filler, now).astype(BF16)
        cols = slice(part * KVW, (part + 1) * KVW)
        out_ref[0:COMMON, cols] = select_rows(chosen, now)[:COMMON]
        out_ref[COMMON:SLOTS, cols] = select_rows(named1, now)
        out_ref[SLOTS : SLOTS + COMMIT, cols] = new[COMMIT:]


def query_order(pos_ref):
    in0 = flag_of(named_slots(pos_ref, 0))
    in1 = flag_of(named_slots(pos_ref, 1))
    never = (1.0 - in0) * (1.0 - in1)
    first = jnp.where(rank_of(never) == lanes(), never, 0.0)
    second = jnp.where(rank_of(in1) + float(BOTH) == lanes(), in1, 0.0)
    return first, second


def queries_kernel(pos_ref, mq_ref, out_ref):
    first, second = query_order(pos_ref)
    picked = select_rows(first + second, mq_ref[...])
    for head in range(HEADS):
        out_ref[head * COMMON : (head + 1) * COMMON, :] = picked[
            :COMMON, head * HEAD : (head + 1) * HEAD
        ]


def attend(q, keys, values, old_acc, old_max):
    scores = lax.dot_general(q, keys, (((1,), (1,)), ((), ())), preferred_element_type=F32)
    new_max = jnp.maximum(old_max, jnp.max(scores, axis=1, keepdims=True))
    weights = jnp.exp2((scores - new_max[:, :1]) * SCALE).astype(BF16)
    keep = jnp.exp2((old_max - new_max) * SCALE)
    gained = jnp.dot(weights, values, preferred_element_type=F32)
    return old_acc * jnp.concatenate([keep, keep], axis=1) + gained, new_max


def lane_block(index):
    return pl.ds(pl.multiple_of(index * HEAD, HEAD), HEAD)


def with_flags(values):
    marked = values > MARK / 2
    zero = jnp.zeros_like(values)
    return jnp.where(marked, zero, values), jnp.where(marked, zero, jnp.ones_like(values))


def gather_rows(refs, block, keys, values):
    at = 0
    for ref in refs:
        flat = len(ref.shape) == 2
        count = ref.shape[0] * (1 if flat else block)
        for index in range(2 * GROUPS):
            cols = slice(index * HEAD, (index + 1) * HEAD)
            if flat:
                got = ref[:, cols]
            else:
                got = ref[:, :block, cols].reshape(count, HEAD)
            rows = slice(at, at + count)
            if index < GROUPS:
                keys[rows, cols] = got
            else:
                first = 2 * (index - GROUPS) * HEAD
                value, flag = with_flags(got)
                values[rows, first : first + HEAD] = value
                values[rows, first + HEAD : first + 2 * HEAD] = flag
        at += count
    spare = keys.shape[0] - at
    if spare:
        keys[at:, :] = keys[:spare, :]
        values[at:, :] = jnp.zeros((spare, PAIR), BF16)


def value_columns(ref, group):
    return ref[:, pl.ds(pl.multiple_of(group * 2 * HEAD, 2 * HEAD), 2 * HEAD)]


def head_rows(group, head):
    return pl.ds(pl.multiple_of((group * PER_GROUP + head) * COMMON, COMMIT), COMMON)


def piece_kernel(first, span, count, *refs):
    refs = list(refs)
    q_ref = refs.pop(0)
    state = [] if first else [refs.pop(0), refs.pop(0)]
    pieces = [refs.pop(0) for _ in range(count)]
    acc, top = refs.pop(0), refs.pop(0)
    old, new = (refs.pop(0), refs.pop(0)) if span else (None, None)
    keys, values = refs
    gather_rows(pieces, COMMON, keys, values)
    at = 0
    for piece in pieces if span else ():
        blocks = piece.shape[0]
        old[at : at + blocks] = piece[:, COMMON:SLOTS, :]
        new[at : at + blocks] = piece[:, SLOTS:, :]
        at += blocks

    def one_group(group, _):
        for head in range(PER_GROUP):
            rows = head_rows(group, head)
            if first:
                before = jnp.zeros((COMMON, 2 * HEAD), F32), jnp.full((COMMON, HEAD), -1e30, F32)
            else:
                before = state[0][rows, :], state[1][rows, :]
            acc[rows, :], top[rows, :] = attend(
                q_ref[rows, :],
                keys[:, lane_block(group)],
                value_columns(values, group),
                *before,
            )
        return 0

    lax.fori_loop(0, GROUPS, one_group, 0)


def estimate(keys):
    work = HEADS * COMMON * keys
    return pl.CostEstimate(
        flops=8 * work * HEAD, bytes_accessed=keys * PAIR * 2, transcendentals=work
    )


STATE = (
    jax.ShapeDtypeStruct((HEADS * COMMON, 2 * HEAD), F32),
    jax.ShapeDtypeStruct((HEADS * COMMON, HEAD), F32),
)
ANY = pl.BlockSpec(memory_space=pltpu.HBM)


def attend_piece(name, queries, state, pieces, span=False):
    rows = [piece.shape[0] * (COMMON if span else 1) for piece in pieces]
    outs = list(STATE)
    if span:
        blocks = sum(piece.shape[0] for piece in pieces)
        outs += [jax.ShapeDtypeStruct((blocks, COMMIT, PAIR), BF16)] * 2
    got = pl.pallas_call(
        functools.partial(piece_kernel, not state, span, len(pieces)),
        out_shape=outs,
        in_specs=[VMEM] * (1 + len(state) + len(pieces)),
        out_specs=[VMEM] * len(outs),
        scratch_shapes=[
            pltpu.VMEM((pl.cdiv(sum(rows), HEAD) * HEAD, KVW), BF16),
            pltpu.VMEM((pl.cdiv(sum(rows), HEAD) * HEAD, PAIR), BF16),
        ],
        input_output_aliases={1: 0, 2: 1} if state else {},
        compiler_params=vmem_params(24),
        cost_estimate=estimate(sum(rows)),
        name=name,
    )(queries, *state, *pieces)
    return tuple(got[:2]), got[2:]


def last_kernel(count, extra_count, *refs):
    refs = list(refs)
    len_ref, pos_ref, q_ref, acc, top = [refs.pop(0) for _ in range(5)]
    sources = [[refs.pop(0) for _ in range(n)] for n in (count, extra_count, extra_count)]
    out_ref, rows_out = refs.pop(0), refs.pop(0)
    held = [(refs.pop(0), refs.pop(0)) for _ in range(3)]
    for source, (keys, values) in zip(sources, held):
        gather_rows(source, COMMIT, keys, values)
    rows_out[:, COMMON:, :] = jnp.zeros((2, COMMIT, HEADS * HEAD), BF16)

    def one_group(group, _):
        for head in range(PER_GROUP):
            rows = head_rows(group, head)
            q = q_ref[rows, :]
            common = acc[rows, :], top[rows, :]
            for number, (keys, values) in enumerate(held):
                full = attend(q, keys[:, lane_block(group)], value_columns(values, group), *common)
                if number == 0:
                    common = full
                    continue
                rows_out[number - 1, :COMMON, lane_block(group * PER_GROUP + head)] = (
                    full[0][:, :HEAD] / full[0][:, HEAD:]
                ).astype(BF16)
        return 0

    lax.fori_loop(0, GROUPS, one_group, 0)
    first, second = query_order(pos_ref)
    live = lax.broadcasted_iota(jnp.int32, (SLOTS, SLOTS), 0) < len_ref[0]
    for number in range(2):
        place = jnp.where(live, first + second if number == 0 else first, 0.0).astype(BF16)
        out_ref[number] = jnp.dot(
            place, rows_out[number], preferred_element_type=F32
        ).astype(BF16)


def attend_last(span_len, commit_pos, queries, state, pieces, olds, news):
    extra = sum(part.shape[0] for part in olds) * COMMIT
    sizes = [sum(piece.shape[0] for piece in pieces), extra, extra]
    return pl.pallas_call(
        functools.partial(last_kernel, len(pieces), len(olds)),
        out_shape=jax.ShapeDtypeStruct((2, SLOTS, HEADS * HEAD), BF16),
        in_specs=[SMEM] + [VMEM] * (4 + len(pieces) + 2 * len(olds)),
        out_specs=VMEM,
        scratch_shapes=[pltpu.VMEM((2, SLOTS, HEADS * HEAD), BF16)]
        + [pltpu.VMEM((size, width), BF16) for size in sizes for width in (KVW, PAIR)],
        compiler_params=vmem_params(24),
        cost_estimate=estimate(sum(sizes)),
        name="attend_last",
    )(span_len, commit_pos, queries, *state, *pieces, *olds, *news)


def in_hbm(x):
    return pltpu.with_memory_space_constraint(x, pltpu.HBM)


NZ, NY = 8, 4


def hop(x, dz, dy):
    pairs = [
        (z * NY + y, (z + dz) % NZ * NY + (y + dy) % NY) for z in range(NZ) for y in range(NY)
    ]
    return lax.ppermute(x, "blk", pairs)


def per_device(
    ctx_keys,
    ctx_values,
    middle_queries,
    span_keys,
    span_values,
    span_len,
    commit_pos,
    commit_emb,
    w_key,
    w_value,
):
    together = lax.optimization_barrier
    ctx = pl.pallas_call(
        join_kernel,
        out_shape=jax.ShapeDtypeStruct((SLOTS, PAIR), BF16),
        in_specs=[ANY, ANY],
        out_specs=VMEM,
        scratch_shapes=[pltpu.SemaphoreType.DMA((2,))],
        compiler_params=vmem_params(4),
        name="join",
    )(in_hbm(ctx_keys), in_hbm(ctx_values))
    near = [hop(ctx, 0, 1), hop(ctx, 0, -1), hop(ctx, 0, 2)]
    held = [in_hbm(x) for x in (commit_emb, w_key, w_value, span_keys, span_values)]
    span = pl.pallas_call(
        prepare_kernel,
        out_shape=jax.ShapeDtypeStruct((SLOTS + COMMIT, PAIR), BF16),
        in_specs=[SMEM, VMEM] + [ANY] * len(held),
        out_specs=VMEM,
        scratch_shapes=[pltpu.VMEM(x.shape, x.dtype) for x in held]
        + [pltpu.SemaphoreType.DMA((len(held),))],
        compiler_params=vmem_params(12),
        name="prepare",
    )(span_len, commit_pos, *held)
    queries = pl.pallas_call(
        queries_kernel,
        out_shape=jax.ShapeDtypeStruct((HEADS * COMMON, HEAD), BF16),
        in_specs=[VMEM, VMEM],
        out_specs=VMEM,
        compiler_params=vmem_params(24),
        name="queries",
    )(commit_pos, middle_queries)

    up1, down1 = hop(span, 1, 0), hop(span, -1, 0)
    up2, down2 = hop(up1, 1, 0), hop(down1, -1, 0)
    up3, down3 = hop(up2, 1, 0), hop(down2, -1, 0)
    far = hop(up3, 1, 0)

    def round_y(x, cut):
        cut = cut * (SLOTS + COMMIT)
        up, down = hop(x, 0, 1), hop(x, 0, -1)
        rest = [hop(up[:cut], 0, 1), hop(down[cut:], 0, -1)]
        return [p.reshape(-1, SLOTS + COMMIT, PAIR) for p in [x, up, down] + rest]

    ctx4 = jnp.concatenate([ctx] + near)
    one = round_y(jnp.concatenate([span, up1, down1, up2, down2]), 3)
    two = round_y(jnp.concatenate([up3, down3, far]), 1)
    half = ctx4.shape[0] // 2
    state, _ = attend_piece("attend_ctx0", queries, (), [ctx4])
    next_up, next_down = hop(ctx4, 1, 0), hop(ctx4, -1, 0)
    next_up, next_down, state = together((next_up, next_down, state))
    last_up, last_down = next_up, next_down
    next_up, next_down = hop(last_up, 1, 0), hop(last_down, -1, 0)
    state, _ = attend_piece("attend_ctx1", queries, state, [last_up, last_down])
    next_up, next_down, state = together((next_up, next_down, state))
    last_up, last_down = next_up, next_down
    next_up, next_down = hop(last_up, 1, 0), hop(last_down, -1, 0)
    state, extra1 = attend_piece("attend_span1", queries, state, one[:3], True)
    state, _ = attend_piece("attend_ctx2", queries, state, [last_up, last_down])
    next_up, next_down, state = together((next_up, next_down, state))
    ends = [hop(next_up[:half], 1, 0), hop(next_down[half:], -1, 0)]
    state, extra2 = attend_piece("attend_span2", queries, state, one[3:] + two[:1], True)
    state, _ = attend_piece("attend_ctx3", queries, state, [next_up, next_down])
    state, extra3 = attend_piece("attend_span3", queries, state, two[1:], True)
    olds = [extra[0] for extra in (extra1, extra2, extra3)]
    news = [extra[1] for extra in (extra1, extra2, extra3)]
    return attend_last(span_len, commit_pos, queries, state, ends, olds, news)


def solution(mesh):
    both = ("file", "blk")
    in_specs = (
        P(both, None),
        P(both, None),
        P(both, None),
        P(both, None),
        P(both, None),
        P(both),
        P(both, None, None),
        P(both, None, None, None),
        P(),
        P(),
    )
    return jax.shard_map(
        per_device, mesh=mesh, in_specs=in_specs, out_specs=P(None, both, None), check_vma=False
    )
```

```python
import functools
import math

import jax
import jax.numpy as jnp
from jax import lax
from jax.experimental import pallas as pl
from jax.experimental.pallas import tpu as pltpu
from jax.sharding import PartitionSpec as P

BF16 = jnp.bfloat16
F32 = jnp.float32
HEAD = 128
GROUPS = 2
PER_GROUP = 7
HEADS = GROUPS * PER_GROUP
COMMIT = 16
SLOTS = 128
COMMON = SLOTS - COMMIT
BOTH = SLOTS - 2 * COMMIT
KVW = GROUPS * HEAD
PAIR = 2 * KVW
ROWS = PER_GROUP * COMMON
MARK = 1e30
SCALE = math.log2(math.e) / math.sqrt(HEAD)
VMEM = pl.BlockSpec(memory_space=pltpu.VMEM)
SMEM = pl.BlockSpec(memory_space=pltpu.SMEM)


def vmem_params(mib):
    return pltpu.CompilerParams(vmem_limit_bytes=mib << 20)


def named_slots(pos_ref, step):
    slot = lax.broadcasted_iota(jnp.int32, (SLOTS, COMMIT), 0)
    return (slot == pos_ref[0, step : step + 1, :]).astype(F32)


def rank_of(flag):
    row = lax.broadcasted_iota(jnp.int32, (SLOTS, SLOTS), 0)
    col = lax.broadcasted_iota(jnp.int32, (SLOTS, SLOTS), 1)
    return jnp.dot((col < row).astype(BF16), flag.astype(BF16), preferred_element_type=F32)


def lanes():
    return lax.broadcasted_iota(jnp.int32, (SLOTS, SLOTS), 1).astype(F32)


def flag_of(named):
    return jnp.broadcast_to(jnp.max(named, axis=1, keepdims=True), (SLOTS, SLOTS))


def select_rows(chosen, rows):
    return lax.dot_general(
        chosen.astype(BF16), rows, (((0,), (0,)), ((), ())), preferred_element_type=F32
    ).astype(BF16)


def join_kernel(keys_ref, values_ref, out_ref, sems):
    copies = [
        pltpu.make_async_copy(keys_ref, out_ref.at[:, pl.ds(0, KVW)], sems.at[0]),
        pltpu.make_async_copy(values_ref, out_ref.at[:, pl.ds(KVW, KVW)], sems.at[1]),
    ]
    for copy in copies:
        copy.start()
    for copy in copies:
        copy.wait()


def prepare_kernel(len_ref, pos_ref, *refs):
    sources, out_ref, held, sems = refs[:5], refs[5], refs[6:11], refs[11]
    copies = [
        pltpu.make_async_copy(source, target, sems.at[i])
        for i, (source, target) in enumerate(zip(sources, held))
    ]
    for copy in copies:
        copy.start()
    emb_ref, wk_ref, wv_ref, sk_ref, sv_ref = held
    named0 = named_slots(pos_ref, 0)
    named1 = named_slots(pos_ref, 1)
    in0 = flag_of(named0)
    stay = 1.0 - flag_of(named1)
    chosen = jnp.where(rank_of(stay) == lanes(), stay, 0.0)
    dead = lax.broadcasted_iota(jnp.int32, (SLOTS, KVW), 0) >= len_ref[0]
    for part, (w_ref, s_ref) in enumerate(((wk_ref, sk_ref), (wv_ref, sv_ref))):
        if part == 0:
            copies[0].wait()
        copies[1 + part].wait()
        copies[3 + part].wait()
        emb = emb_ref[0].reshape(2 * COMMIT, emb_ref.shape[3])
        new = jnp.dot(emb, w_ref[...], preferred_element_type=F32).astype(BF16)
        put = jnp.dot(named0.astype(BF16), new[:COMMIT], preferred_element_type=F32)
        now = jnp.where(
            jnp.concatenate([in0, in0], axis=1) > 0.5, put, s_ref[...].astype(F32)
        )
        filler = now[0:1, :] if part == 0 else jnp.full((1, KVW), MARK, F32)
        now = jnp.where(dead, filler, now).astype(BF16)
        cols = slice(part * KVW, (part + 1) * KVW)
        out_ref[0:COMMON, cols] = select_rows(chosen, now)[:COMMON]
        out_ref[COMMON:SLOTS, cols] = select_rows(named1, now)
        out_ref[SLOTS : SLOTS + COMMIT, cols] = new[COMMIT:]


def query_order(pos_ref):
    in0 = flag_of(named_slots(pos_ref, 0))
    in1 = flag_of(named_slots(pos_ref, 1))
    never = (1.0 - in0) * (1.0 - in1)
    first = jnp.where(rank_of(never) == lanes(), never, 0.0)
    second = jnp.where(rank_of(in1) + float(BOTH) == lanes(), in1, 0.0)
    return first, second


def queries_kernel(pos_ref, mq_ref, out_ref):
    first, second = query_order(pos_ref)
    picked = select_rows(first + second, mq_ref[...])
    for head in range(HEADS):
        out_ref[head * COMMON : (head + 1) * COMMON, :] = picked[
            :COMMON, head * HEAD : (head + 1) * HEAD
        ]


def attend(q, keys, values, old_acc, old_max):
    scores = lax.dot_general(q, keys, (((1,), (1,)), ((), ())), preferred_element_type=F32)
    new_max = jnp.maximum(old_max, jnp.max(scores, axis=1, keepdims=True))
    weights = jnp.exp2((scores - new_max[:, :1]) * SCALE).astype(BF16)
    keep = jnp.exp2((old_max - new_max) * SCALE)
    gained = jnp.dot(weights, values, preferred_element_type=F32)
    return old_acc * jnp.concatenate([keep, keep], axis=1) + gained, new_max


def lane_block(index):
    return pl.ds(pl.multiple_of(index * HEAD, HEAD), HEAD)


def with_flags(values):
    marked = values > MARK / 2
    zero = jnp.zeros_like(values)
    return jnp.where(marked, zero, values), jnp.where(marked, zero, jnp.ones_like(values))


def gather_rows(refs, block, keys, values):
    at = 0
    for ref in refs:
        flat = len(ref.shape) == 2
        count = ref.shape[0] * (1 if flat else block)
        for index in range(2 * GROUPS):
            cols = slice(index * HEAD, (index + 1) * HEAD)
            if flat:
                got = ref[:, cols]
            else:
                got = ref[:, :block, cols].reshape(count, HEAD)
            rows = slice(at, at + count)
            if index < GROUPS:
                keys[rows, cols] = got
            else:
                first = 2 * (index - GROUPS) * HEAD
                value, flag = with_flags(got)
                values[rows, first : first + HEAD] = value
                values[rows, first + HEAD : first + 2 * HEAD] = flag
        at += count
    spare = keys.shape[0] - at
    if spare:
        keys[at:, :] = keys[:spare, :]
        values[at:, :] = jnp.zeros((spare, PAIR), BF16)


def value_block(group):
    return pl.ds(pl.multiple_of(group * 2 * HEAD, 2 * HEAD), 2 * HEAD)


def head_rows(group, head):
    return pl.ds(pl.multiple_of((group * PER_GROUP + head) * COMMON, COMMIT), COMMON)


TILES = ((0, 400), (400, 384))
LIMIT = 1e30


def gained(q_ref, keys, values, top, rows):
    scores = lax.dot_general(
        q_ref[rows, :], keys, (((1,), (1,)), ((), ())), preferred_element_type=F32
    )
    weights = jnp.exp2((scores - top[rows, :][:, :1]) * SCALE).astype(BF16)
    return jnp.dot(weights, values, preferred_element_type=F32)


def tile_rows(group, start, size):
    return pl.ds(pl.multiple_of(group * ROWS + start, COMMIT), size)


def too_large(total):
    return jnp.max(jnp.where(total < LIMIT, 0.0, 1.0)) > 0.5


def first_kernel(q_ref, piece, acc, top, keys, values):
    gather_rows([piece], COMMON, keys, values)

    def one_group(group, _):
        for head in range(PER_GROUP):
            rows = head_rows(group, head)
            acc[rows, :], top[rows, :] = attend(
                q_ref[rows, :],
                keys[:, lane_block(group)],
                values[:, value_block(group)],
                jnp.zeros((COMMON, 2 * HEAD), F32),
                jnp.full((COMMON, HEAD), -1e30, F32),
            )
        return 0

    lax.fori_loop(0, GROUPS, one_group, 0)


def piece_kernel(span, count, *refs):
    refs = list(refs)
    q_ref, acc_in, top_in = [refs.pop(0) for _ in range(3)]
    pieces = [refs.pop(0) for _ in range(count)]
    acc, top = refs.pop(0), refs.pop(0)
    old, new = (refs.pop(0), refs.pop(0)) if span else (None, None)
    keys, values = refs
    gather_rows(pieces, COMMON, keys, values)
    at = 0
    for piece in pieces if span else ():
        blocks = piece.shape[0]
        old[at : at + blocks] = piece[:, COMMON:SLOTS, :]
        new[at : at + blocks] = piece[:, SLOTS:, :]
        at += blocks

    def one_group(group, _):
        for start, size in TILES:
            rows = tile_rows(group, start, size)
            acc[rows, :] = acc_in[rows, :] + gained(
                q_ref, keys[:, lane_block(group)], values[:, value_block(group)], top_in, rows
            )
        return 0

    lax.fori_loop(0, GROUPS, one_group, 0)
    again = too_large(acc[:, HEAD:])
    top[...] = top_in[...]

    @pl.when(again)
    def _():
        def one_head(index, _):
            group = index // PER_GROUP
            rows = head_rows(0, index)
            acc[rows, :], top[rows, :] = attend(
                q_ref[rows, :],
                keys[:, lane_block(group)],
                values[:, value_block(group)],
                acc_in[rows, :],
                top_in[rows, :],
            )
            return 0

        lax.fori_loop(0, HEADS, one_head, 0)


def estimate(keys):
    work = HEADS * COMMON * keys
    return pl.CostEstimate(
        flops=8 * work * HEAD, bytes_accessed=keys * PAIR * 2, transcendentals=work
    )


STATE = (
    jax.ShapeDtypeStruct((HEADS * COMMON, 2 * HEAD), F32),
    jax.ShapeDtypeStruct((HEADS * COMMON, HEAD), F32),
)
ANY = pl.BlockSpec(memory_space=pltpu.HBM)


def padded(rows):
    return [
        pltpu.VMEM((pl.cdiv(rows, HEAD) * HEAD, width), BF16) for width in (KVW, PAIR)
    ]


def attend_first(queries, piece):
    return pl.pallas_call(
        first_kernel,
        out_shape=STATE,
        in_specs=[VMEM] * 2,
        out_specs=[VMEM] * 2,
        scratch_shapes=padded(piece.shape[0]),
        compiler_params=vmem_params(24),
        cost_estimate=estimate(piece.shape[0]),
        name="attend_first",
    )(queries, piece)


def attend_piece(name, queries, state, pieces, span=False):
    rows = sum(piece.shape[0] for piece in pieces) * (COMMON if span else 1)
    outs = list(STATE)
    if span:
        outs += [jax.ShapeDtypeStruct((rows // COMMON, COMMIT, PAIR), BF16)] * 2
    got = pl.pallas_call(
        functools.partial(piece_kernel, span, len(pieces)),
        out_shape=outs,
        in_specs=[VMEM] * (3 + len(pieces)),
        out_specs=[VMEM] * len(outs),
        scratch_shapes=padded(rows),
        compiler_params=vmem_params(24),
        cost_estimate=estimate(rows),
        name=name,
    )(queries, *state, *pieces)
    return tuple(got[:2]), got[2:]


def ratio(full):
    return (full[:, :HEAD] / full[:, HEAD:]).astype(BF16)


def last_kernel(count, extra_count, *refs):
    refs = list(refs)
    len_ref, pos_ref, q_ref, acc, top = [refs.pop(0) for _ in range(5)]
    sources = [[refs.pop(0) for _ in range(n)] for n in (count, extra_count, extra_count)]
    out_ref, rows_out, done, largest = [refs.pop(0) for _ in range(4)]
    held = [(refs.pop(0), refs.pop(0)) for _ in range(3)]
    for source, (keys, values) in zip(sources, held):
        gather_rows(source, COMMIT, keys, values)
    rows_out[:, COMMON:, :] = jnp.zeros((2, COMMIT, HEADS * HEAD), BF16)

    def one_group(group, _):
        for start, size in TILES:
            rows = tile_rows(group, start, size)
            adds = [
                gained(q_ref, keys[:, lane_block(group)], values[:, value_block(group)], top, rows)
                for keys, values in held
            ]
            common = acc[rows, :] + adds[0]
            for number in range(2):
                full = common + adds[1 + number]
                done[number, rows, :] = ratio(full)
                largest[number, rows, :] = full[:, HEAD:]
        return 0

    lax.fori_loop(0, GROUPS, one_group, 0)

    @pl.when(too_large(largest[...]))
    def _():
        def one_head(index, _):
            group = index // PER_GROUP
            rows = head_rows(0, index)
            state = acc[rows, :], top[rows, :]
            for number, (keys, values) in enumerate(held):
                full = attend(
                    q_ref[rows, :], keys[:, lane_block(group)], values[:, value_block(group)], *state
                )
                if number == 0:
                    state = full
                else:
                    done[number - 1, rows, :] = ratio(full[0])
            return 0

        lax.fori_loop(0, HEADS, one_head, 0)

    first, second = query_order(pos_ref)
    live = lax.broadcasted_iota(jnp.int32, (SLOTS, SLOTS), 0) < len_ref[0]
    for number in range(2):
        for head in range(HEADS):
            rows_out[number, :COMMON, head * HEAD : (head + 1) * HEAD] = done[
                number, head * COMMON : (head + 1) * COMMON, :
            ]
        place = jnp.where(live, first + second if number == 0 else first, 0.0).astype(BF16)
        out_ref[number] = jnp.dot(
            place, rows_out[number], preferred_element_type=F32
        ).astype(BF16)


def attend_last(span_len, commit_pos, queries, state, pieces, olds, news):
    extra = sum(part.shape[0] for part in olds) * COMMIT
    sizes = [sum(piece.shape[0] for piece in pieces), extra, extra]
    return pl.pallas_call(
        functools.partial(last_kernel, len(pieces), len(olds)),
        out_shape=jax.ShapeDtypeStruct((2, SLOTS, HEADS * HEAD), BF16),
        in_specs=[SMEM] + [VMEM] * (4 + len(pieces) + 2 * len(olds)),
        out_specs=VMEM,
        scratch_shapes=[
            pltpu.VMEM((2, SLOTS, HEADS * HEAD), BF16),
            pltpu.VMEM((2, HEADS * COMMON, HEAD), BF16),
            pltpu.VMEM((2, HEADS * COMMON, HEAD), F32),
        ]
        + [scratch for size in sizes for scratch in padded(size)],
        compiler_params=vmem_params(24),
        cost_estimate=estimate(sum(sizes)),
        name="attend_last",
    )(span_len, commit_pos, queries, *state, *pieces, *olds, *news)


def in_hbm(x):
    return pltpu.with_memory_space_constraint(x, pltpu.HBM)


NZ, NY = 8, 4


def exchange(x, partner):
    pairs = []
    for z in range(NZ):
        for y in range(NY):
            pz, py = partner(z, y)
            pairs.append((z * NY + y, pz % NZ * NY + py % NY))
    return lax.ppermute(x, "blk", pairs)


def side(i, odd):
    return i + 1 if i % 2 == odd else i - 1


def z_even(x):
    return exchange(x, lambda z, y: (side(z, 0), y))


def z_odd(x):
    return exchange(x, lambda z, y: (side(z, 1), y))


def y_even(x):
    return exchange(x, lambda z, y: (z, side(y, 0)))


def y_odd(x):
    return exchange(x, lambda z, y: (z, side(y, 1)))


def y_far(x):
    return exchange(x, lambda z, y: (z, y + 2))


def round_z(even, odd):
    return z_even(odd), z_odd(even)


def per_device(
    ctx_keys,
    ctx_values,
    middle_queries,
    span_keys,
    span_values,
    span_len,
    commit_pos,
    commit_emb,
    w_key,
    w_value,
):
    together = lax.optimization_barrier
    ctx = pl.pallas_call(
        join_kernel,
        out_shape=jax.ShapeDtypeStruct((SLOTS, PAIR), BF16),
        in_specs=[ANY, ANY],
        out_specs=VMEM,
        scratch_shapes=[pltpu.SemaphoreType.DMA((2,))],
        compiler_params=vmem_params(4),
        name="join",
    )(in_hbm(ctx_keys), in_hbm(ctx_values))
    near = [y_even(ctx), y_odd(ctx), y_far(ctx)]
    held = [in_hbm(x) for x in (commit_emb, w_key, w_value, span_keys, span_values)]
    span = pl.pallas_call(
        prepare_kernel,
        out_shape=jax.ShapeDtypeStruct((SLOTS + COMMIT, PAIR), BF16),
        in_specs=[SMEM, VMEM] + [ANY] * len(held),
        out_specs=VMEM,
        scratch_shapes=[pltpu.VMEM(x.shape, x.dtype) for x in held]
        + [pltpu.SemaphoreType.DMA((len(held),))],
        compiler_params=vmem_params(12),
        name="prepare",
    )(span_len, commit_pos, *held)
    queries = pl.pallas_call(
        queries_kernel,
        out_shape=jax.ShapeDtypeStruct((HEADS * COMMON, HEAD), BF16),
        in_specs=[VMEM, VMEM],
        out_specs=VMEM,
        compiler_params=vmem_params(24),
        name="queries",
    )(commit_pos, middle_queries)

    near1 = round_z(span, span)
    near2 = round_z(*near1)

    def blocks(x):
        return x.reshape(-1, SLOTS + COMMIT, PAIR)

    ctx4 = jnp.concatenate([ctx] + near)
    state = attend_first(queries, ctx4)
    *near2, state = together((*near2, state))
    near3 = round_z(*near2)
    far = z_even(near3[1])
    first = jnp.concatenate([span, *near1, *near2])
    second = jnp.concatenate([*near3, far])
    first_y = y_even(first), y_odd(first)
    ctx1 = round_z(ctx4, ctx4)
    *ctx1, state = together((*ctx1, state))
    ctx2 = round_z(*ctx1)
    state, _ = attend_piece("attend_ctx1", queries, state, ctx1)
    *first_y, state = together((*first_y, state))
    cut = 3 * (SLOTS + COMMIT)
    first_far = y_even(first_y[1][:cut]), y_odd(first_y[0][cut:])
    *ctx2, state = together((*ctx2, state))
    ctx3 = round_z(*ctx2)
    second_y = y_even(second), y_odd(second)
    state, extra1 = attend_piece(
        "attend_span1", queries, state, [blocks(x) for x in (first, *first_y)], True
    )
    state, _ = attend_piece("attend_ctx2", queries, state, ctx2)
    second_y, ctx3, state = together((second_y, ctx3, state))
    cut = SLOTS + COMMIT
    second_far = y_even(second_y[1][:cut]), y_odd(second_y[0][cut:])
    ends = [z_even(ctx3[1])]
    state, extra2 = attend_piece(
        "attend_span2", queries, state, [blocks(x) for x in (*first_far, second)], True
    )
    state, _ = attend_piece("attend_ctx3", queries, state, ctx3)
    state, extra3 = attend_piece(
        "attend_span3", queries, state, [blocks(x) for x in (*second_y, *second_far)], True
    )
    olds = [extra[0] for extra in (extra1, extra2, extra3)]
    news = [extra[1] for extra in (extra1, extra2, extra3)]
    return attend_last(span_len, commit_pos, queries, state, ends, olds, news)


def solution(mesh):
    both = ("file", "blk")
    in_specs = (
        P(both, None),
        P(both, None),
        P(both, None),
        P(both, None),
        P(both, None),
        P(both),
        P(both, None, None),
        P(both, None, None, None),
        P(),
        P(),
    )
    return jax.shard_map(
        per_device, mesh=mesh, in_specs=in_specs, out_specs=P(None, both, None), check_vma=False
    )
```

```python
import functools
import math

import jax
import jax.numpy as jnp
from jax import lax
from jax.experimental import pallas as pl
from jax.experimental.pallas import tpu as pltpu
from jax.sharding import PartitionSpec as P

BF16 = jnp.bfloat16
F32 = jnp.float32
HEAD = 128
GROUPS = 2
PER_GROUP = 7
HEADS = GROUPS * PER_GROUP
COMMIT = 16
SLOTS = 128
COMMON = SLOTS - COMMIT
BOTH = SLOTS - 2 * COMMIT
KVW = GROUPS * HEAD
PAIR = 2 * KVW
ROWS = PER_GROUP * COMMON
MARK = 1e30
SCALE = math.log2(math.e) / math.sqrt(HEAD)
VMEM = pl.BlockSpec(memory_space=pltpu.VMEM)
SMEM = pl.BlockSpec(memory_space=pltpu.SMEM)


def vmem_params(mib):
    return pltpu.CompilerParams(vmem_limit_bytes=mib << 20)


def named_slots(pos_ref, step):
    slot = lax.broadcasted_iota(jnp.int32, (SLOTS, COMMIT), 0)
    return (slot == pos_ref[0, step : step + 1, :]).astype(F32)


def rank_of(flag):
    row = lax.broadcasted_iota(jnp.int32, (SLOTS, SLOTS), 0)
    col = lax.broadcasted_iota(jnp.int32, (SLOTS, SLOTS), 1)
    return jnp.dot((col < row).astype(BF16), flag.astype(BF16), preferred_element_type=F32)


def lanes():
    return lax.broadcasted_iota(jnp.int32, (SLOTS, SLOTS), 1).astype(F32)


def flag_of(named):
    return jnp.broadcast_to(jnp.max(named, axis=1, keepdims=True), (SLOTS, SLOTS))


def select_rows(chosen, rows):
    return lax.dot_general(
        chosen.astype(BF16), rows, (((0,), (0,)), ((), ())), preferred_element_type=F32
    ).astype(BF16)


def join_kernel(keys_ref, values_ref, out_ref, sems):
    copies = [
        pltpu.make_async_copy(keys_ref, out_ref.at[:, pl.ds(0, KVW)], sems.at[0]),
        pltpu.make_async_copy(values_ref, out_ref.at[:, pl.ds(KVW, KVW)], sems.at[1]),
    ]
    for copy in copies:
        copy.start()
    for copy in copies:
        copy.wait()


def prepare_kernel(len_ref, pos_ref, *refs):
    sources, out_ref, held, sems = refs[:5], refs[5], refs[6:11], refs[11]
    copies = [
        pltpu.make_async_copy(source, target, sems.at[i])
        for i, (source, target) in enumerate(zip(sources, held))
    ]
    for copy in copies:
        copy.start()
    emb_ref, wk_ref, wv_ref, sk_ref, sv_ref = held
    named0 = named_slots(pos_ref, 0)
    named1 = named_slots(pos_ref, 1)
    in0 = flag_of(named0)
    stay = 1.0 - flag_of(named1)
    chosen = jnp.where(rank_of(stay) == lanes(), stay, 0.0)
    dead = lax.broadcasted_iota(jnp.int32, (SLOTS, KVW), 0) >= len_ref[0]
    for part, (w_ref, s_ref) in enumerate(((wk_ref, sk_ref), (wv_ref, sv_ref))):
        if part == 0:
            copies[0].wait()
        copies[1 + part].wait()
        copies[3 + part].wait()
        emb = emb_ref[0].reshape(2 * COMMIT, emb_ref.shape[3])
        new = jnp.dot(emb, w_ref[...], preferred_element_type=F32).astype(BF16)
        put = jnp.dot(named0.astype(BF16), new[:COMMIT], preferred_element_type=F32)
        now = jnp.where(
            jnp.concatenate([in0, in0], axis=1) > 0.5, put, s_ref[...].astype(F32)
        )
        filler = now[0:1, :] if part == 0 else jnp.full((1, KVW), MARK, F32)
        now = jnp.where(dead, filler, now).astype(BF16)
        cols = slice(part * KVW, (part + 1) * KVW)
        out_ref[0:COMMON, cols] = select_rows(chosen, now)[:COMMON]
        out_ref[COMMON:SLOTS, cols] = select_rows(named1, now)
        out_ref[SLOTS : SLOTS + COMMIT, cols] = new[COMMIT:]


def query_order(pos_ref):
    in0 = flag_of(named_slots(pos_ref, 0))
    in1 = flag_of(named_slots(pos_ref, 1))
    never = (1.0 - in0) * (1.0 - in1)
    first = jnp.where(rank_of(never) == lanes(), never, 0.0)
    second = jnp.where(rank_of(in1) + float(BOTH) == lanes(), in1, 0.0)
    return first, second


def queries_kernel(pos_ref, mq_ref, out_ref):
    first, second = query_order(pos_ref)
    picked = select_rows(first + second, mq_ref[...])
    for head in range(HEADS):
        out_ref[head * COMMON : (head + 1) * COMMON, :] = picked[
            :COMMON, head * HEAD : (head + 1) * HEAD
        ]


def attend(q, keys, values, old_acc, old_max):
    scores = lax.dot_general(q, keys, (((1,), (1,)), ((), ())), preferred_element_type=F32)
    new_max = jnp.maximum(old_max, jnp.max(scores, axis=1, keepdims=True))
    weights = jnp.exp2((scores - new_max[:, :1]) * SCALE).astype(BF16)
    keep = jnp.exp2((old_max - new_max) * SCALE)
    gained = jnp.dot(weights, values, preferred_element_type=F32)
    return old_acc * jnp.concatenate([keep, keep], axis=1) + gained, new_max


def lane_block(index):
    return pl.ds(pl.multiple_of(index * HEAD, HEAD), HEAD)


def with_flags(values):
    marked = values > MARK / 2
    zero = jnp.zeros_like(values)
    return jnp.where(marked, zero, values), jnp.where(marked, zero, jnp.ones_like(values))


def gather_rows(refs, start, block, keys, values):
    at = 0
    for ref in refs:
        flat = len(ref.shape) == 2
        count = ref.shape[0] * (1 if flat else block)
        for index in range(2 * GROUPS):
            cols = slice(index * HEAD, (index + 1) * HEAD)
            if flat:
                got = ref[:, cols]
            else:
                got = ref[:, start : start + block, cols].reshape(count, HEAD)
            rows = slice(at, at + count)
            if index < GROUPS:
                keys[rows, cols] = got
            else:
                first = 2 * (index - GROUPS) * HEAD
                value, flag = with_flags(got)
                values[rows, first : first + HEAD] = value
                values[rows, first + HEAD : first + 2 * HEAD] = flag
        at += count
    spare = keys.shape[0] - at
    if spare:
        keys[at:, :] = keys[:spare, :]
        values[at:, :] = jnp.zeros((spare, PAIR), BF16)


def value_block(group):
    return pl.ds(pl.multiple_of(group * 2 * HEAD, 2 * HEAD), 2 * HEAD)


def head_rows(group, head):
    return pl.ds(pl.multiple_of((group * PER_GROUP + head) * COMMON, COMMIT), COMMON)


TILES = ((0, 400), (400, 384))
LIMIT = 1e30


def gained(q_ref, keys, values, top, rows):
    scores = lax.dot_general(
        q_ref[rows, :], keys, (((1,), (1,)), ((), ())), preferred_element_type=F32
    )
    weights = jnp.exp2((scores - top[rows, :][:, :1]) * SCALE).astype(BF16)
    return jnp.dot(weights, values, preferred_element_type=F32)


def tile_rows(group, start, size):
    return pl.ds(pl.multiple_of(group * ROWS + start, COMMIT), size)


def too_large(total):
    return jnp.max(jnp.where(total < LIMIT, 0.0, 1.0)) > 0.5


def first_kernel(q_ref, *refs):
    *pieces, acc, top, keys, values = refs
    gather_rows(pieces, 0, COMMON, keys, values)

    def one_group(group, _):
        for head in range(PER_GROUP):
            rows = head_rows(group, head)
            acc[rows, :], top[rows, :] = attend(
                q_ref[rows, :],
                keys[:, lane_block(group)],
                values[:, value_block(group)],
                jnp.zeros((COMMON, 2 * HEAD), F32),
                jnp.full((COMMON, HEAD), -1e30, F32),
            )
        return 0

    lax.fori_loop(0, GROUPS, one_group, 0)


def piece_kernel(span, count, *refs):
    refs = list(refs)
    q_ref, acc_in, top_in = [refs.pop(0) for _ in range(3)]
    pieces = [refs.pop(0) for _ in range(count)]
    acc, top = refs.pop(0), refs.pop(0)
    old, new = (refs.pop(0), refs.pop(0)) if span else (None, None)
    keys, values = refs
    gather_rows(pieces, 0, COMMON, keys, values)
    at = 0
    for piece in pieces:
        if len(piece.shape) == 2:
            continue
        blocks = piece.shape[0]
        old[at : at + blocks] = piece[:, COMMON:SLOTS, :]
        new[at : at + blocks] = piece[:, SLOTS:, :]
        at += blocks

    def one_group(group, _):
        for start, size in TILES:
            rows = tile_rows(group, start, size)
            acc[rows, :] = acc_in[rows, :] + gained(
                q_ref, keys[:, lane_block(group)], values[:, value_block(group)], top_in, rows
            )
        return 0

    lax.fori_loop(0, GROUPS, one_group, 0)
    again = too_large(acc[:, HEAD:])
    top[...] = top_in[...]

    @pl.when(again)
    def _():
        def one_head(index, _):
            group = index // PER_GROUP
            rows = head_rows(0, index)
            acc[rows, :], top[rows, :] = attend(
                q_ref[rows, :],
                keys[:, lane_block(group)],
                values[:, value_block(group)],
                acc_in[rows, :],
                top_in[rows, :],
            )
            return 0

        lax.fori_loop(0, HEADS, one_head, 0)


def estimate(keys):
    work = HEADS * COMMON * keys
    return pl.CostEstimate(
        flops=14 * work * HEAD, bytes_accessed=keys * PAIR * 2, transcendentals=work
    )


STATE = (
    jax.ShapeDtypeStruct((HEADS * COMMON, 2 * HEAD), F32),
    jax.ShapeDtypeStruct((HEADS * COMMON, HEAD), F32),
)
ANY = pl.BlockSpec(memory_space=pltpu.HBM)


def padded(rows):
    return [
        pltpu.VMEM((pl.cdiv(rows, HEAD) * HEAD, width), BF16) for width in (KVW, PAIR)
    ]


def attend_first(queries, pieces):
    rows = sum(piece.shape[0] for piece in pieces)
    return pl.pallas_call(
        first_kernel,
        out_shape=STATE,
        in_specs=[VMEM] * (1 + len(pieces)),
        out_specs=[VMEM] * 2,
        scratch_shapes=padded(rows),
        compiler_params=vmem_params(24),
        cost_estimate=estimate(rows),
        name="attend_first",
    )(queries, *pieces)


def attend_piece(name, queries, state, pieces):
    blocks = sum(piece.shape[0] for piece in pieces if len(piece.shape) == 3)
    rows = blocks * COMMON + sum(piece.shape[0] for piece in pieces if len(piece.shape) == 2)
    outs = list(STATE)
    if blocks:
        outs += [jax.ShapeDtypeStruct((blocks, COMMIT, PAIR), BF16)] * 2
    got = pl.pallas_call(
        functools.partial(piece_kernel, blocks > 0, len(pieces)),
        out_shape=outs,
        in_specs=[VMEM] * (3 + len(pieces)),
        out_specs=[VMEM] * len(outs),
        scratch_shapes=padded(rows),
        compiler_params=vmem_params(24),
        cost_estimate=estimate(rows),
        name=name,
    )(queries, *state, *pieces)
    return tuple(got[:2]), got[2:]


def ratio(full):
    return (full[:, :HEAD] / full[:, HEAD:]).astype(BF16)


def last_kernel(count, extra_count, *refs):
    refs = list(refs)
    len_ref, pos_ref, q_ref, acc, top = [refs.pop(0) for _ in range(5)]
    sources = [[refs.pop(0) for _ in range(n)] for n in (count, extra_count, extra_count)]
    out_ref, rows_out, done, largest = [refs.pop(0) for _ in range(4)]
    held = [(refs.pop(0), refs.pop(0)) for _ in range(3)]
    ends = sources[0]
    spans = ((0, COMMON), (COMMON, COMMIT), (SLOTS, COMMIT))
    for source, (start, size), (keys, values) in zip(sources, spans, held):
        at = 0
        if start:
            at = sum(ref.shape[0] for ref in source) * COMMIT
            gather_rows(source, 0, COMMIT, keys.at[:at], values.at[:at])
        gather_rows(ends, start, size, keys.at[at:], values.at[at:])
    rows_out[:, COMMON:, :] = jnp.zeros((2, COMMIT, HEADS * HEAD), BF16)

    def one_group(group, _):
        for start, size in TILES:
            rows = tile_rows(group, start, size)
            adds = [
                gained(q_ref, keys[:, lane_block(group)], values[:, value_block(group)], top, rows)
                for keys, values in held
            ]
            common = acc[rows, :] + adds[0]
            for number in range(2):
                full = common + adds[1 + number]
                done[number, rows, :] = ratio(full)
                largest[number, rows, :] = full[:, HEAD:]
        return 0

    lax.fori_loop(0, GROUPS, one_group, 0)

    @pl.when(too_large(largest[...]))
    def _():
        def one_head(index, _):
            group = index // PER_GROUP
            rows = head_rows(0, index)
            state = acc[rows, :], top[rows, :]
            for number, (keys, values) in enumerate(held):
                full = attend(
                    q_ref[rows, :], keys[:, lane_block(group)], values[:, value_block(group)], *state
                )
                if number == 0:
                    state = full
                else:
                    done[number - 1, rows, :] = ratio(full[0])
            return 0

        lax.fori_loop(0, HEADS, one_head, 0)

    first, second = query_order(pos_ref)
    live = lax.broadcasted_iota(jnp.int32, (SLOTS, SLOTS), 0) < len_ref[0]
    for number in range(2):
        for head in range(HEADS):
            rows_out[number, :COMMON, head * HEAD : (head + 1) * HEAD] = done[
                number, head * COMMON : (head + 1) * COMMON, :
            ]
        place = jnp.where(live, first + second if number == 0 else first, 0.0).astype(BF16)
        out_ref[number] = jnp.dot(
            place, rows_out[number], preferred_element_type=F32
        ).astype(BF16)


def attend_last(span_len, commit_pos, queries, state, pieces, olds, news):
    blocks = sum(piece.shape[0] for piece in pieces)
    extra = (blocks + sum(part.shape[0] for part in olds)) * COMMIT
    sizes = [blocks * COMMON, extra, extra]
    return pl.pallas_call(
        functools.partial(last_kernel, len(pieces), len(olds)),
        out_shape=jax.ShapeDtypeStruct((2, SLOTS, HEADS * HEAD), BF16),
        in_specs=[SMEM] + [VMEM] * (4 + len(pieces) + 2 * len(olds)),
        out_specs=VMEM,
        scratch_shapes=[
            pltpu.VMEM((2, SLOTS, HEADS * HEAD), BF16),
            pltpu.VMEM((2, HEADS * COMMON, HEAD), BF16),
            pltpu.VMEM((2, HEADS * COMMON, HEAD), F32),
        ]
        + [scratch for size in sizes for scratch in padded(size)],
        compiler_params=vmem_params(24),
        cost_estimate=estimate(sum(sizes)),
        name="attend_last",
    )(span_len, commit_pos, queries, *state, *pieces, *olds, *news)


def in_hbm(x):
    return pltpu.with_memory_space_constraint(x, pltpu.HBM)


NZ, NY = 8, 4


def exchange(x, partner):
    pairs = []
    for z in range(NZ):
        for y in range(NY):
            pz, py = partner(z, y)
            pairs.append((z * NY + y, pz % NZ * NY + py % NY))
    return lax.ppermute(x, "blk", pairs)


def side(i, odd):
    return i + 1 if i % 2 == odd else i - 1


def z_even(x):
    return exchange(x, lambda z, y: (side(z, 0), y))


def z_odd(x):
    return exchange(x, lambda z, y: (side(z, 1), y))


def y_even(x):
    return exchange(x, lambda z, y: (z, side(y, 0)))


def y_odd(x):
    return exchange(x, lambda z, y: (z, side(y, 1)))


def y_far(x):
    return exchange(x, lambda z, y: (z, y + 2))


def round_z(even, odd):
    return z_even(odd), z_odd(even)


def per_device(
    ctx_keys,
    ctx_values,
    middle_queries,
    span_keys,
    span_values,
    span_len,
    commit_pos,
    commit_emb,
    w_key,
    w_value,
):
    together = lax.optimization_barrier
    ctx = pl.pallas_call(
        join_kernel,
        out_shape=jax.ShapeDtypeStruct((SLOTS, PAIR), BF16),
        in_specs=[ANY, ANY],
        out_specs=VMEM,
        scratch_shapes=[pltpu.SemaphoreType.DMA((2,))],
        compiler_params=vmem_params(4),
        name="join",
    )(in_hbm(ctx_keys), in_hbm(ctx_values))
    ring1 = round_z(ctx, ctx)
    held = [in_hbm(x) for x in (commit_emb, w_key, w_value, span_keys, span_values)]
    span = pl.pallas_call(
        prepare_kernel,
        out_shape=jax.ShapeDtypeStruct((SLOTS + COMMIT, PAIR), BF16),
        in_specs=[SMEM, VMEM] + [ANY] * len(held),
        out_specs=VMEM,
        scratch_shapes=[pltpu.VMEM(x.shape, x.dtype) for x in held]
        + [pltpu.SemaphoreType.DMA((len(held),))],
        compiler_params=vmem_params(12),
        cost_estimate=pl.CostEstimate(flops=1 << 28, bytes_accessed=12 << 20, transcendentals=0),
        name="prepare",
    )(span_len, commit_pos, *held)
    queries = pl.pallas_call(
        queries_kernel,
        out_shape=jax.ShapeDtypeStruct((HEADS * COMMON, HEAD), BF16),
        in_specs=[VMEM, VMEM],
        out_specs=VMEM,
        compiler_params=vmem_params(24),
        name="queries",
    )(commit_pos, middle_queries)

    def blocks(x):
        return x.reshape(-1, SLOTS + COMMIT, PAIR)

    ring1, span = together((ring1, span))
    ring2 = round_z(*ring1)
    near = [y_even(span), y_odd(span), y_far(span)]
    ring3 = round_z(*ring2)
    span4 = jnp.concatenate([span] + near)
    span1 = round_z(span4, span4)
    state = attend_first(queries, [*ring1, *ring2])
    ring4 = z_even(ring3[1])
    column = jnp.concatenate([ctx, *ring1, *ring2, *ring3, ring4])
    beside = y_even(column), y_odd(column)
    span1, state = together((span1, state))
    span2 = round_z(*span1)
    state, extra0 = attend_piece(
        "attend_mixed", queries, state, [ctx, *ring3, ring4, blocks(span4)]
    )
    span2, state = together((span2, state))
    span3 = round_z(*span2)
    state, extra1 = attend_piece("attend_span1", queries, state, [blocks(x) for x in span1])
    beside, state = together((beside, state))
    half = column.shape[0] // 2
    across = y_even(beside[1][:half]), y_odd(beside[0][half:])
    state, _ = attend_piece("attend_ctx1", queries, state, [beside[0]])
    state, _ = attend_piece("attend_ctx2", queries, state, [beside[1]])
    state, extra2 = attend_piece("attend_span2", queries, state, [blocks(x) for x in span2])
    span3, state = together((span3, state))
    half = span4.shape[0] // 2
    ends = z_even(span3[1][:half]), z_odd(span3[0][half:])
    state, _ = attend_piece("attend_ctx3", queries, state, across)
    state, extra3 = attend_piece("attend_span3", queries, state, [blocks(x) for x in span3])
    olds = [extra[0] for extra in (extra0, extra1, extra2, extra3)]
    news = [extra[1] for extra in (extra0, extra1, extra2, extra3)]
    ends = [blocks(x) for x in ends]
    return attend_last(span_len, commit_pos, queries, state, ends, olds, news)


def solution(mesh):
    both = ("file", "blk")
    in_specs = (
        P(both, None),
        P(both, None),
        P(both, None),
        P(both, None),
        P(both, None),
        P(both),
        P(both, None, None),
        P(both, None, None, None),
        P(),
        P(),
    )
    return jax.shard_map(
        per_device, mesh=mesh, in_specs=in_specs, out_specs=P(None, both, None), check_vma=False
    )
```

```python
import functools
import math

import jax
import jax.numpy as jnp
from jax import lax
from jax.experimental import pallas as pl
from jax.experimental.pallas import tpu as pltpu
from jax.sharding import PartitionSpec as P

BF16 = jnp.bfloat16
F32 = jnp.float32
HEAD = 128
GROUPS = 2
PER_GROUP = 7
HEADS = GROUPS * PER_GROUP
COMMIT = 16
SLOTS = 128
COMMON = SLOTS - COMMIT
BOTH = SLOTS - 2 * COMMIT
KVW = GROUPS * HEAD
PAIR = 2 * KVW
ROWS = PER_GROUP * COMMON
MARK = 1e30
SCALE = math.log2(math.e) / math.sqrt(HEAD)
VMEM = pl.BlockSpec(memory_space=pltpu.VMEM)
SMEM = pl.BlockSpec(memory_space=pltpu.SMEM)


def vmem_params(mib):
    return pltpu.CompilerParams(vmem_limit_bytes=mib << 20)


def named_slots(pos_ref, step):
    slot = lax.broadcasted_iota(jnp.int32, (SLOTS, COMMIT), 0)
    return (slot == pos_ref[0, step : step + 1, :]).astype(F32)


def rank_of(flag):
    row = lax.broadcasted_iota(jnp.int32, (SLOTS, SLOTS), 0)
    col = lax.broadcasted_iota(jnp.int32, (SLOTS, SLOTS), 1)
    return jnp.dot((col < row).astype(BF16), flag.astype(BF16), preferred_element_type=F32)


def lanes():
    return lax.broadcasted_iota(jnp.int32, (SLOTS, SLOTS), 1).astype(F32)


def flag_of(named):
    return jnp.broadcast_to(jnp.max(named, axis=1, keepdims=True), (SLOTS, SLOTS))


def select_rows(chosen, rows):
    return lax.dot_general(
        chosen.astype(BF16), rows, (((0,), (0,)), ((), ())), preferred_element_type=F32
    ).astype(BF16)


def join_kernel(keys_ref, values_ref, out_ref, sems):
    copies = [
        pltpu.make_async_copy(keys_ref, out_ref.at[:, pl.ds(0, KVW)], sems.at[0]),
        pltpu.make_async_copy(values_ref, out_ref.at[:, pl.ds(KVW, KVW)], sems.at[1]),
    ]
    for copy in copies:
        copy.start()
    for copy in copies:
        copy.wait()


def prepare_kernel(len_ref, pos_ref, *refs):
    sources, out_ref, held, sems = refs[:5], refs[5], refs[6:11], refs[11]
    copies = [
        pltpu.make_async_copy(source, target, sems.at[i])
        for i, (source, target) in enumerate(zip(sources, held))
    ]
    for copy in copies:
        copy.start()
    emb_ref, wk_ref, wv_ref, sk_ref, sv_ref = held
    named0 = named_slots(pos_ref, 0)
    named1 = named_slots(pos_ref, 1)
    in0 = flag_of(named0)
    stay = 1.0 - flag_of(named1)
    chosen = jnp.where(rank_of(stay) == lanes(), stay, 0.0)
    dead = lax.broadcasted_iota(jnp.int32, (SLOTS, KVW), 0) >= len_ref[0]
    for part, (w_ref, s_ref) in enumerate(((wk_ref, sk_ref), (wv_ref, sv_ref))):
        if part == 0:
            copies[0].wait()
        copies[1 + part].wait()
        copies[3 + part].wait()
        emb = emb_ref[0].reshape(2 * COMMIT, emb_ref.shape[3])
        new = jnp.dot(emb, w_ref[...], preferred_element_type=F32).astype(BF16)
        put = jnp.dot(named0.astype(BF16), new[:COMMIT], preferred_element_type=F32)
        now = jnp.where(
            jnp.concatenate([in0, in0], axis=1) > 0.5, put, s_ref[...].astype(F32)
        )
        filler = now[0:1, :] if part == 0 else jnp.full((1, KVW), MARK, F32)
        now = jnp.where(dead, filler, now).astype(BF16)
        cols = slice(part * KVW, (part + 1) * KVW)
        out_ref[0:COMMON, cols] = select_rows(chosen, now)[:COMMON]
        out_ref[COMMON:SLOTS, cols] = select_rows(named1, now)
        out_ref[SLOTS : SLOTS + COMMIT, cols] = new[COMMIT:]


def query_order(pos_ref):
    in0 = flag_of(named_slots(pos_ref, 0))
    in1 = flag_of(named_slots(pos_ref, 1))
    never = (1.0 - in0) * (1.0 - in1)
    first = jnp.where(rank_of(never) == lanes(), never, 0.0)
    second = jnp.where(rank_of(in1) + float(BOTH) == lanes(), in1, 0.0)
    return first, second


def queries_kernel(pos_ref, mq_ref, out_ref):
    first, second = query_order(pos_ref)
    picked = select_rows(first + second, mq_ref[...])
    for head in range(HEADS):
        out_ref[head * COMMON : (head + 1) * COMMON, :] = picked[
            :COMMON, head * HEAD : (head + 1) * HEAD
        ]


def attend(q, keys, values, old_acc, old_max):
    scores = lax.dot_general(q, keys, (((1,), (1,)), ((), ())), preferred_element_type=F32)
    new_max = jnp.maximum(old_max, jnp.max(scores, axis=1, keepdims=True))
    weights = jnp.exp2((scores - new_max[:, :1]) * SCALE).astype(BF16)
    keep = jnp.exp2((old_max - new_max) * SCALE)
    gained = jnp.dot(weights, values, preferred_element_type=F32)
    return old_acc * jnp.concatenate([keep, keep], axis=1) + gained, new_max


def lane_block(index):
    return pl.ds(pl.multiple_of(index * HEAD, HEAD), HEAD)


def with_flags(values):
    marked = values > MARK / 2
    zero = jnp.zeros_like(values)
    return jnp.where(marked, zero, values), jnp.where(marked, zero, jnp.ones_like(values))


def gather_rows(refs, start, block, keys, values):
    at = 0
    for ref in refs:
        flat = len(ref.shape) == 2
        count = ref.shape[0] * (1 if flat else block)
        for index in range(2 * GROUPS):
            cols = slice(index * HEAD, (index + 1) * HEAD)
            if flat:
                got = ref[:, cols]
            else:
                got = ref[:, start : start + block, cols].reshape(count, HEAD)
            rows = slice(at, at + count)
            if index < GROUPS:
                keys[rows, cols] = got
            else:
                first = 2 * (index - GROUPS) * HEAD
                value, flag = with_flags(got)
                values[rows, first : first + HEAD] = value
                values[rows, first + HEAD : first + 2 * HEAD] = flag
        at += count
    spare = keys.shape[0] - at
    if spare:
        keys[at:, :] = keys[:spare, :]
        values[at:, :] = jnp.zeros((spare, PAIR), BF16)


def value_block(group):
    return pl.ds(pl.multiple_of(group * 2 * HEAD, 2 * HEAD), 2 * HEAD)


def head_rows(group, head):
    return pl.ds(pl.multiple_of((group * PER_GROUP + head) * COMMON, COMMIT), COMMON)


TILES = ((0, 400), (400, 384))
LIMIT = 1e30


def gained(q_ref, keys, values, top, rows):
    scores = lax.dot_general(
        q_ref[rows, :], keys, (((1,), (1,)), ((), ())), preferred_element_type=F32
    )
    weights = jnp.exp2((scores - top[rows, :][:, :1]) * SCALE).astype(BF16)
    return jnp.dot(weights, values, preferred_element_type=F32)


def tile_rows(group, start, size):
    return pl.ds(pl.multiple_of(group * ROWS + start, COMMIT), size)


def too_large(total):
    return jnp.max(jnp.where(total < LIMIT, 0.0, 1.0)) > 0.5


def first_kernel(q_ref, *refs):
    *pieces, acc, top, keys, values = refs
    gather_rows(pieces, 0, COMMON, keys, values)

    def one_group(group, _):
        for head in range(PER_GROUP):
            rows = head_rows(group, head)
            acc[rows, :], top[rows, :] = attend(
                q_ref[rows, :],
                keys[:, lane_block(group)],
                values[:, value_block(group)],
                jnp.zeros((COMMON, 2 * HEAD), F32),
                jnp.full((COMMON, HEAD), -1e30, F32),
            )
        return 0

    lax.fori_loop(0, GROUPS, one_group, 0)


def piece_kernel(span, count, *refs):
    refs = list(refs)
    q_ref, acc_in, top_in = [refs.pop(0) for _ in range(3)]
    pieces = [refs.pop(0) for _ in range(count)]
    acc, top = refs.pop(0), refs.pop(0)
    old, new = (refs.pop(0), refs.pop(0)) if span else (None, None)
    keys, values = refs
    gather_rows(pieces, 0, COMMON, keys, values)
    at = 0
    for piece in pieces:
        if len(piece.shape) == 2:
            continue
        blocks = piece.shape[0]
        old[at : at + blocks] = piece[:, COMMON:SLOTS, :]
        new[at : at + blocks] = piece[:, SLOTS:, :]
        at += blocks

    def one_group(group, _):
        for start, size in TILES:
            rows = tile_rows(group, start, size)
            acc[rows, :] = acc_in[rows, :] + gained(
                q_ref, keys[:, lane_block(group)], values[:, value_block(group)], top_in, rows
            )
        return 0

    lax.fori_loop(0, GROUPS, one_group, 0, unroll=True)
    again = too_large(acc[:, HEAD:])
    top[...] = top_in[...]

    @pl.when(again)
    def _():
        def one_head(index, _):
            group = index // PER_GROUP
            rows = head_rows(0, index)
            acc[rows, :], top[rows, :] = attend(
                q_ref[rows, :],
                keys[:, lane_block(group)],
                values[:, value_block(group)],
                acc_in[rows, :],
                top_in[rows, :],
            )
            return 0

        lax.fori_loop(0, HEADS, one_head, 0)


def estimate(keys):
    work = HEADS * COMMON * keys
    return pl.CostEstimate(
        flops=14 * work * HEAD, bytes_accessed=keys * PAIR * 2, transcendentals=work
    )


STATE = (
    jax.ShapeDtypeStruct((HEADS * COMMON, 2 * HEAD), F32),
    jax.ShapeDtypeStruct((HEADS * COMMON, HEAD), F32),
)
ANY = pl.BlockSpec(memory_space=pltpu.HBM)


def padded(rows):
    return [
        pltpu.VMEM((pl.cdiv(rows, HEAD) * HEAD, width), BF16) for width in (KVW, PAIR)
    ]


def attend_first(queries, pieces):
    rows = sum(piece.shape[0] for piece in pieces)
    return pl.pallas_call(
        first_kernel,
        out_shape=STATE,
        in_specs=[VMEM] * (1 + len(pieces)),
        out_specs=[VMEM] * 2,
        scratch_shapes=padded(rows),
        compiler_params=vmem_params(24),
        cost_estimate=estimate(rows),
        name="attend_first",
    )(queries, *pieces)


def attend_piece(name, queries, state, pieces):
    blocks = sum(piece.shape[0] for piece in pieces if len(piece.shape) == 3)
    rows = blocks * COMMON + sum(piece.shape[0] for piece in pieces if len(piece.shape) == 2)
    outs = list(STATE)
    if blocks:
        outs += [jax.ShapeDtypeStruct((blocks, COMMIT, PAIR), BF16)] * 2
    got = pl.pallas_call(
        functools.partial(piece_kernel, blocks > 0, len(pieces)),
        out_shape=outs,
        in_specs=[VMEM] * (3 + len(pieces)),
        out_specs=[VMEM] * len(outs),
        scratch_shapes=padded(rows),
        compiler_params=vmem_params(24),
        cost_estimate=estimate(rows),
        name=name,
    )(queries, *state, *pieces)
    return tuple(got[:2]), got[2:]


def ratio(full):
    return (full[:, :HEAD] / full[:, HEAD:]).astype(BF16)


def last_kernel(count, extra_count, *refs):
    refs = list(refs)
    len_ref, pos_ref, q_ref, acc, top = [refs.pop(0) for _ in range(5)]
    sources = [[refs.pop(0) for _ in range(n)] for n in (count, extra_count, extra_count)]
    out_ref, rows_out, done, largest = [refs.pop(0) for _ in range(4)]
    held = [(refs.pop(0), refs.pop(0)) for _ in range(3)]
    ends = sources[0]
    spans = ((0, COMMON), (COMMON, COMMIT), (SLOTS, COMMIT))
    for source, (start, size), (keys, values) in zip(sources, spans, held):
        at = 0
        if start:
            at = sum(ref.shape[0] for ref in source) * COMMIT
            gather_rows(source, 0, COMMIT, keys.at[:at], values.at[:at])
        gather_rows(ends, start, size, keys.at[at:], values.at[at:])
    rows_out[:, COMMON:, :] = jnp.zeros((2, COMMIT, HEADS * HEAD), BF16)

    def one_group(group, _):
        for start, size in TILES:
            rows = tile_rows(group, start, size)
            adds = [
                gained(q_ref, keys[:, lane_block(group)], values[:, value_block(group)], top, rows)
                for keys, values in held
            ]
            common = acc[rows, :] + adds[0]
            for number in range(2):
                full = common + adds[1 + number]
                done[number, rows, :] = ratio(full)
                largest[number, rows, :] = full[:, HEAD:]
        return 0

    lax.fori_loop(0, GROUPS, one_group, 0, unroll=True)

    @pl.when(too_large(largest[...]))
    def _():
        def one_head(index, _):
            group = index // PER_GROUP
            rows = head_rows(0, index)
            state = acc[rows, :], top[rows, :]
            for number, (keys, values) in enumerate(held):
                full = attend(
                    q_ref[rows, :], keys[:, lane_block(group)], values[:, value_block(group)], *state
                )
                if number == 0:
                    state = full
                else:
                    done[number - 1, rows, :] = ratio(full[0])
            return 0

        lax.fori_loop(0, HEADS, one_head, 0)

    first, second = query_order(pos_ref)
    live = lax.broadcasted_iota(jnp.int32, (SLOTS, SLOTS), 0) < len_ref[0]
    for number in range(2):
        for head in range(HEADS):
            rows_out[number, :COMMON, head * HEAD : (head + 1) * HEAD] = done[
                number, head * COMMON : (head + 1) * COMMON, :
            ]
        place = jnp.where(live, first + second if number == 0 else first, 0.0).astype(BF16)
        out_ref[number] = jnp.dot(
            place, rows_out[number], preferred_element_type=F32
        ).astype(BF16)


def attend_last(span_len, commit_pos, queries, state, pieces, olds, news):
    blocks = sum(piece.shape[0] for piece in pieces)
    extra = (blocks + sum(part.shape[0] for part in olds)) * COMMIT
    sizes = [blocks * COMMON, extra, extra]
    return pl.pallas_call(
        functools.partial(last_kernel, len(pieces), len(olds)),
        out_shape=jax.ShapeDtypeStruct((2, SLOTS, HEADS * HEAD), BF16),
        in_specs=[SMEM] + [VMEM] * (4 + len(pieces) + 2 * len(olds)),
        out_specs=VMEM,
        scratch_shapes=[
            pltpu.VMEM((2, SLOTS, HEADS * HEAD), BF16),
            pltpu.VMEM((2, HEADS * COMMON, HEAD), BF16),
            pltpu.VMEM((2, HEADS * COMMON, HEAD), F32),
        ]
        + [scratch for size in sizes for scratch in padded(size)],
        compiler_params=vmem_params(24),
        cost_estimate=estimate(sum(sizes)),
        name="attend_last",
    )(span_len, commit_pos, queries, *state, *pieces, *olds, *news)


def in_hbm(x):
    return pltpu.with_memory_space_constraint(x, pltpu.HBM)


NZ, NY = 8, 4


def exchange(x, partner):
    pairs = []
    for z in range(NZ):
        for y in range(NY):
            pz, py = partner(z, y)
            pairs.append((z * NY + y, pz % NZ * NY + py % NY))
    return lax.ppermute(x, "blk", pairs)


def side(i, odd):
    return i + 1 if i % 2 == odd else i - 1


def z_even(x):
    return exchange(x, lambda z, y: (side(z, 0), y))


def z_odd(x):
    return exchange(x, lambda z, y: (side(z, 1), y))


def y_even(x):
    return exchange(x, lambda z, y: (z, side(y, 0)))


def y_odd(x):
    return exchange(x, lambda z, y: (z, side(y, 1)))


def y_far(x):
    return exchange(x, lambda z, y: (z, y + 2))


def round_z(even, odd):
    return z_even(odd), z_odd(even)


def per_device(
    ctx_keys,
    ctx_values,
    middle_queries,
    span_keys,
    span_values,
    span_len,
    commit_pos,
    commit_emb,
    w_key,
    w_value,
):
    together = lax.optimization_barrier
    ctx = pl.pallas_call(
        join_kernel,
        out_shape=jax.ShapeDtypeStruct((SLOTS, PAIR), BF16),
        in_specs=[ANY, ANY],
        out_specs=VMEM,
        scratch_shapes=[pltpu.SemaphoreType.DMA((2,))],
        compiler_params=vmem_params(4),
        name="join",
    )(in_hbm(ctx_keys), in_hbm(ctx_values))
    ring1 = round_z(ctx, ctx)
    held = [in_hbm(x) for x in (commit_emb, w_key, w_value, span_keys, span_values)]
    span = pl.pallas_call(
        prepare_kernel,
        out_shape=jax.ShapeDtypeStruct((SLOTS + COMMIT, PAIR), BF16),
        in_specs=[SMEM, VMEM] + [ANY] * len(held),
        out_specs=VMEM,
        scratch_shapes=[pltpu.VMEM(x.shape, x.dtype) for x in held]
        + [pltpu.SemaphoreType.DMA((len(held),))],
        compiler_params=vmem_params(12),
        cost_estimate=pl.CostEstimate(flops=1 << 28, bytes_accessed=12 << 20, transcendentals=0),
        name="prepare",
    )(span_len, commit_pos, *held)
    queries = pl.pallas_call(
        queries_kernel,
        out_shape=jax.ShapeDtypeStruct((HEADS * COMMON, HEAD), BF16),
        in_specs=[VMEM, VMEM],
        out_specs=VMEM,
        compiler_params=vmem_params(24),
        name="queries",
    )(commit_pos, middle_queries)

    def blocks(x):
        return x.reshape(-1, SLOTS + COMMIT, PAIR)

    ring1, span = together((ring1, span))
    ring2 = round_z(*ring1)
    near = [y_even(span), y_odd(span), y_far(span)]
    ring3 = round_z(*ring2)
    span4 = jnp.concatenate([span] + near)
    span1 = round_z(span4, span4)
    state = attend_first(queries, [*ring1, *ring2])
    ring4 = z_even(ring3[1])
    column = jnp.concatenate([ctx, *ring1, *ring2, *ring3, ring4])
    beside = y_even(column), y_odd(column)
    span1, state = together((span1, state))
    span2 = round_z(*span1)
    state, extra0 = attend_piece(
        "attend_mixed", queries, state, [ctx, *ring3, ring4, blocks(span4)]
    )
    span2, state = together((span2, state))
    span3 = round_z(*span2)
    state, extra1 = attend_piece("attend_span1", queries, state, [blocks(x) for x in span1])
    beside, state = together((beside, state))
    half = column.shape[0] // 2
    across = y_even(beside[1][:half]), y_odd(beside[0][half:])
    state, _ = attend_piece("attend_ctx1", queries, state, [beside[0]])
    state, _ = attend_piece("attend_ctx2", queries, state, [beside[1]])
    state, extra2 = attend_piece("attend_span2", queries, state, [blocks(x) for x in span2])
    span3, state = together((span3, state))
    half = span4.shape[0] // 2
    ends = z_even(span3[1][:half]), z_odd(span3[0][half:])
    state, _ = attend_piece("attend_ctx3", queries, state, across)
    state, extra3 = attend_piece("attend_span3", queries, state, [blocks(x) for x in span3])
    olds = [extra[0] for extra in (extra0, extra1, extra2, extra3)]
    news = [extra[1] for extra in (extra0, extra1, extra2, extra3)]
    ends = [blocks(x) for x in ends]
    return attend_last(span_len, commit_pos, queries, state, ends, olds, news)


def solution(mesh):
    both = ("file", "blk")
    in_specs = (
        P(both, None),
        P(both, None),
        P(both, None),
        P(both, None),
        P(both, None),
        P(both),
        P(both, None, None),
        P(both, None, None, None),
        P(),
        P(),
    )
    return jax.shard_map(
        per_device, mesh=mesh, in_specs=in_specs, out_specs=P(None, both, None), check_vma=False
    )
```
